32 devices in a mesh: users: 8 (over z, y), seq: 4 (over x, core).
Axes of the slice: x: 2, y: 2, z: 4, core: 2. Of those that a mesh axis runs over, the one named last changes fastest.
Arguments:
- raw_events: bfloat16 [4, 3072, 512], P('seq', 'users'), may hold values from -6 to 6
- target_user: int32 [4, 3072], P('seq', 'users'), may hold values from 0 to 7, as said below
- target_place: int32 [4, 3072], P('seq', 'users'), may hold values from 0 to 1023, as said below
- send_counts: int32 [4, 8, 8], P('seq', 'users'), may hold values from 0 to 48, as said below
- lengths: int32 [8], P('users'), may hold values from 512 to 1024, as said below
- cotangent: bfloat16 [8, 1024, 512], P('users', 'seq'), may hold values from -0.06591797 to 0.06591797
- encoder_in: bfloat16 [512, 512], replicated, may hold values from -0.25 to 0.25
- encoder_out: bfloat16 [512, 512], replicated, may hold values from -0.25 to 0.25
- proj_weight: bfloat16 [512, 1024], replicated, may hold values from -0.25 to 0.25
- proj_bias: float32 [1024], replicated, may hold values from -3 to 3
- out_weight: bfloat16 [256, 512], replicated, may hold values from -0.375 to 0.375
- out_bias: float32 [512], replicated, may hold values from -3 to 3
Outputs:
- layer_out: bfloat16 [8, 1024, 512], P('users', 'seq')
- grad_proj_weight: bfloat16 [512, 1024], replicated
- grad_proj_bias: float32 [1024], replicated
- grad_out_weight: bfloat16 [256, 512], replicated
- grad_out_bias: float32 [512], replicated
The draws below stay inside these ranges and needn't reach their ends.
Inputs may be any that keep to these rules, and one draw needn't show every extreme that they name: `target_user`: within one ingestion shard the event rows come first, grouped by user in increasing order; the rows after the shard's total of send_counts carry no event. An event of block b has a position in b * 256 to (b + 1) * 256 - 1. The events of a user are exactly its positions 0 to its length - 1, each once. `target_place`: see target_user. send_counts[b, i, u] rows of shard i in block b go to user u; at most 48, and exactly 48 for some shard and user. The counts of a user in block b sum to min(max(length - b * 256, 0), 256). `lengths`: some user has length exactly 1024.
All inputs are finite; a program needn't handle non-finite values.
Results may differ from the reference program's by a relative error of at most 0.0084.
The reference program's roundings to bfloat16 on the way count: a program that leaves them out, or rounds other values in their place, can miss the bound.
Values may be sent and summed in bfloat16 or wider, within the bound.
A program may use at most 64 MiB of HBM per device.

```python
import jax
import jax.numpy as jnp
from jax import lax

D = 512
HEADS = 4
HEAD = 64
F_IN = 512
LS = 256
A = 256
USERS = 8
BLOCKS = 4
L = 1024
CAP = 48
SLOTS = 384
INGEST = 3072
EVENTS = 8192


def event_plan(key):
    lengths = jax.random.randint(jax.random.fold_in(key, 11), (USERS,), L // 2, L + 1, dtype=jnp.int32)
    longest = jax.random.randint(jax.random.fold_in(key, 12), (), 0, USERS, dtype=jnp.int32)
    lengths = lengths.at[longest].set(L)
    block_ids = jnp.arange(BLOCKS, dtype=jnp.int32)
    live_count = jnp.clip(lengths[None, :] - block_ids[:, None] * LS, 0, LS)
    ticket = jnp.arange(SLOTS, dtype=jnp.int32)
    noise = jax.random.randint(jax.random.fold_in(key, 13), (BLOCKS, USERS, SLOTS), 0, 2 ** 19, dtype=jnp.int32)
    chosen = jax.random.randint(jax.random.fold_in(key, 14), (BLOCKS, USERS), 0, USERS, dtype=jnp.int32)
    ranking = noise * SLOTS + ticket[None, None, :]
    ranking = jnp.where((ticket // CAP)[None, None, :] == chosen[:, :, None], ticket[None, None, :] - SLOTS, ranking)
    order = jnp.argsort(ranking, axis=-1)[:, :, :LS].astype(jnp.int32)
    source = order // CAP
    place = jnp.arange(LS, dtype=jnp.int32)
    alive = place[None, None, :] < live_count[:, :, None]
    block_idx = jnp.broadcast_to(block_ids[:, None, None], (BLOCKS, USERS, LS))
    user_idx = jnp.broadcast_to(jnp.arange(USERS, dtype=jnp.int32)[None, :, None], (BLOCKS, USERS, LS))
    counts = jnp.zeros((BLOCKS, USERS, USERS), jnp.int32).at[block_idx, source, user_idx].add(alive.astype(jnp.int32))
    offsets = jnp.cumsum(counts, axis=2) - counts
    per_user = jnp.transpose(counts, (0, 2, 1))
    before = jnp.cumsum(per_user, axis=2) - per_user
    sort_key = jnp.where(alive, source * LS + place[None, None, :], USERS * LS + place[None, None, :])
    inverse = jnp.argsort(jnp.argsort(sort_key, axis=-1), axis=-1).astype(jnp.int32)
    rank = inverse - jnp.take_along_axis(before, source, axis=2)
    row = offsets[block_idx, source, user_idx] + rank
    flat_index = jnp.where(alive, source * SLOTS + row, USERS * SLOTS)
    filler_user = jax.random.randint(jax.random.fold_in(key, 15), (BLOCKS, INGEST), 0, USERS, dtype=jnp.int32)
    filler_place = jax.random.randint(jax.random.fold_in(key, 16), (BLOCKS, INGEST), 0, LS, dtype=jnp.int32)
    filler_place = filler_place + block_ids[:, None] * LS
    target_user = filler_user.at[block_idx, flat_index].set(user_idx, mode='drop')
    target_place = filler_place.at[block_idx, flat_index].set(block_idx * LS + place[None, None, :], mode='drop')
    return (lengths, counts, target_user, target_place)


def draw_target_user(key, part):
    return event_plan(key)[2]


def draw_target_place(key, part):
    return event_plan(key)[3]


def draw_send_counts(key, part):
    return event_plan(key)[1]


def draw_lengths(key, part):
    return event_plan(key)[0]


def strengthened(values, key, source, target, blocks, factor):
    def block_of(axis_at):
        return (jnp.arange(values.shape[axis_at]) // (values.shape[axis_at] // blocks)).reshape((-1,) + (1,) * (values.ndim - 1 - axis_at))

    one_side = jax.random.permutation(key, blocks)[block_of(target)]
    other_side = (block_of(target) + blocks // 2) % blocks
    return jnp.where((block_of(source) == one_side) | (block_of(source) == other_side), factor * values, values)


def block_scale(key, shape, pieces, smallest, top_value):
    factor_of, own = 1.0, jax.random.fold_in(key, 6)
    for dim, parts in pieces:
        heights = jnp.exp(jax.random.uniform(jax.random.fold_in(own, dim), (parts,), jnp.float32, smallest / len(pieces), top_value / len(pieces)))
        factor_of = factor_of * jnp.repeat(heights, shape[dim] // parts).reshape([-1 if axis == dim else 1 for axis in range(len(shape))])
    return factor_of


def scatter_about(rng, dims, scale, reach, shards=(), kind=jnp.bfloat16):
    factor_of = block_scale(rng, dims, shards, -0.22, 0.18) if shards else 1.0
    drawn = jax.random.normal(rng, dims, jnp.float32) * scale * factor_of
    return jnp.minimum(jnp.maximum(drawn, -reach), reach).astype(kind)


def bell_draw_with(rng, dims, spread, most, shards, heavy, kind=jnp.bfloat16):
    drawn = spread * jax.random.normal(rng, dims, jnp.float32)
    if shards:
        drawn = drawn * block_scale(rng, dims, shards, -0.22, 0.18)
    return jnp.clip(strengthened(drawn, jax.random.fold_in(rng, 3), *heavy), -most, most).astype(kind)


def setup_inputs(seed: int = 0) -> dict:
    arg_keys = jax.random.split(jax.random.key(seed), 13)
    raw_events = scatter_about(arg_keys[0], (BLOCKS, INGEST, F_IN), 1.0, 6.0, ((0, 4), (1, 8)))
    target_user = draw_target_user(jax.random.fold_in(arg_keys[12], 71), 0)
    target_place = draw_target_place(jax.random.fold_in(arg_keys[12], 71), 0)
    send_counts = draw_send_counts(jax.random.fold_in(arg_keys[12], 71), 0)
    lengths = draw_lengths(jax.random.fold_in(arg_keys[12], 71), 0)
    cotangent = bell_draw_with(arg_keys[5], (USERS, L, D), (EVENTS ** -0.5), 0.06591797, ((0, 8), (1, 4)), (0, 2, 8, 2.0))
    encoder_in = scatter_about(arg_keys[6], (F_IN, D), F_IN ** -0.5, 0.25)
    encoder_out = scatter_about(arg_keys[7], (D, D), D ** -0.5, 0.25)
    proj_weight = scatter_about(arg_keys[8], (D, 4 * A), D ** -0.5, 0.25)
    proj_bias = scatter_about(arg_keys[9], (4 * A,), 0.5, 3.0, (), jnp.float32)
    out_weight = scatter_about(arg_keys[10], (A, D), A ** -0.5, 0.375)
    out_bias = scatter_about(arg_keys[11], (D,), 0.5, 3.0, (), jnp.float32)
    return dict(raw_events=raw_events, target_user=target_user, target_place=target_place, send_counts=send_counts, lengths=lengths, cotangent=cotangent, encoder_in=encoder_in, encoder_out=encoder_out, proj_weight=proj_weight, proj_bias=proj_bias, out_weight=out_weight, out_bias=out_bias)


EPSILON = 1e-05

def layer_norm(values):
    center = values - lax.optimization_barrier(jnp.mean(values, axis=-1, keepdims=True))
    inverse = lax.rsqrt(lax.optimization_barrier(jnp.mean(center * center, axis=-1, keepdims=True)) + EPSILON)
    return (center * inverse, inverse)

def silu_grad(values):
    sigmoid = jax.nn.sigmoid(values)
    return sigmoid * (1.0 + values * (1.0 - sigmoid))

def one_user(sequence, user_cot, length, proj_weight, proj_bias, out_weight, out_bias):
    width = HEADS * HEAD
    score_scale = HEAD ** (-0.5)
    positions = jnp.arange(L, dtype=jnp.int32)
    present = positions < length
    normed = layer_norm(sequence.astype(jnp.float32))[0].astype(jnp.bfloat16)
    projected = jnp.dot(normed, proj_weight, preferred_element_type=jnp.float32) + proj_bias
    gates = jax.nn.silu(projected).astype(jnp.bfloat16)
    gate_u = gates[:, :width].astype(jnp.float32)
    value_heads = gates[:, width:2 * width].reshape(L, HEADS, HEAD).astype(jnp.float32)
    query_heads = gates[:, 2 * width:3 * width].reshape(L, HEADS, HEAD).astype(jnp.float32)
    key_heads = gates[:, 3 * width:].reshape(L, HEADS, HEAD).astype(jnp.float32)
    scores = jnp.einsum('qhd,khd->hqk', query_heads, key_heads) * score_scale
    allowed = (positions[None, :] <= positions[:, None]) & (positions[None, :] < length)
    weights = jnp.where(allowed, jax.nn.silu(scores), 0.0).astype(jnp.bfloat16)
    weights_wide = weights.astype(jnp.float32)
    attended = jnp.einsum('hqk,khd->qhd', weights_wide, value_heads).reshape(L, width)
    onorm, inverse = layer_norm(attended)
    mixed = (onorm * gate_u).astype(jnp.bfloat16)
    result = jnp.dot(mixed, out_weight, preferred_element_type=jnp.float32) + out_bias + sequence.astype(jnp.float32)
    layer_out = jnp.where(present[:, None], result, 0.0).astype(jnp.bfloat16)
    d_out = jnp.where(present[:, None], user_cot, jnp.zeros_like(user_cot))
    grad_ob = lax.optimization_barrier(jnp.sum(d_out.astype(jnp.float32), axis=0))
    grad_ow = jnp.dot(mixed.T, d_out, preferred_element_type=jnp.float32)
    d_mixed = jnp.dot(d_out, out_weight.T, preferred_element_type=jnp.float32)
    d_gate_u = d_mixed * onorm
    d_onorm = d_mixed * gate_u
    d_att = (d_onorm - lax.optimization_barrier(jnp.mean(d_onorm, axis=-1, keepdims=True)) - onorm * lax.optimization_barrier(jnp.mean(d_onorm * onorm, axis=-1, keepdims=True))) * inverse
    d_att = d_att.astype(jnp.bfloat16)
    d_heads = d_att.reshape(L, HEADS, HEAD).astype(jnp.float32)
    d_weights = jnp.einsum('qhd,khd->hqk', d_heads, value_heads)
    d_values = jnp.einsum('hqk,qhd->khd', weights_wide, d_heads).reshape(L, width)
    d_scores = jnp.where(allowed, d_weights * silu_grad(scores), 0.0).astype(jnp.bfloat16).astype(jnp.float32)
    d_queries = score_scale * jnp.einsum('hqk,khd->qhd', d_scores, key_heads).reshape(L, width)
    d_keys = score_scale * jnp.einsum('hqk,qhd->khd', d_scores, query_heads).reshape(L, width)
    d_proj = jnp.concatenate([d_gate_u, d_values, d_queries, d_keys], axis=1) * silu_grad(projected)
    d_proj = d_proj.astype(jnp.bfloat16)
    grad_pb = lax.optimization_barrier(jnp.sum(d_proj.astype(jnp.float32), axis=0))
    grad_pw = jnp.dot(normed.T, d_proj, preferred_element_type=jnp.float32)
    return (layer_out, grad_pw, grad_pb, grad_ow, grad_ob)

def reference(raw_events, target_user, target_place, send_counts, lengths, cotangent, encoder_in, encoder_out, proj_weight, proj_bias, out_weight, out_bias):
    flat_raw = raw_events.reshape(BLOCKS * INGEST, F_IN)
    enc_hidden = jax.nn.silu(jnp.dot(flat_raw, encoder_in, preferred_element_type=jnp.float32)).astype(jnp.bfloat16)
    encoded = jnp.dot(enc_hidden, encoder_out, preferred_element_type=jnp.float32).astype(jnp.bfloat16)
    totals = lax.optimization_barrier(jnp.sum(send_counts, axis=2))
    row_ids = jnp.arange(INGEST, dtype=jnp.int32)
    shard_of = row_ids // SLOTS
    valid = (row_ids % SLOTS)[None, :] < totals[:, shard_of]
    flat_index = jnp.where(valid, target_user * L + target_place, USERS * L).astype(jnp.int32).reshape(-1)
    sequences = jnp.zeros((USERS * L, D), jnp.bfloat16).at[flat_index].set(encoded, mode='drop')
    sequences = sequences.reshape(USERS, L, D)
    width = HEADS * HEAD
    initial = (jnp.zeros((D, 4 * width), jnp.float32), jnp.zeros((4 * width,), jnp.float32), jnp.zeros((width, D), jnp.float32), jnp.zeros((D,), jnp.float32))

    def advance(running, inputs):
        sequence, user_cot, length = inputs
        layer_out, grad_pw, grad_pb, grad_ow, grad_ob = one_user(sequence, user_cot, length, proj_weight, proj_bias, out_weight, out_bias)
        running = (running[0] + grad_pw, running[1] + grad_pb, running[2] + grad_ow, running[3] + grad_ob)
        return (running, layer_out)
    running, outputs = lax.scan(advance, initial, (sequences, cotangent, lengths))
    return (outputs, running[0].astype(jnp.bfloat16), running[1], running[2].astype(jnp.bfloat16), running[3])
```

```python
import functools

import jax
import jax.numpy as jnp
from jax import lax
from jax.experimental import pallas as pl
from jax.experimental.pallas import tpu as pltpu
from jax.sharding import PartitionSpec as P

HEAD = 64
EPSILON = 1e-05
LANES = 128
ROWS = 16
F32 = jnp.float32
BF16 = jnp.bfloat16


def sigmoid(values):
    return 0.5 * jnp.tanh(0.5 * values) + 0.5


def silu(values):
    return values * sigmoid(values)


def silu_grad(values):
    gate = sigmoid(values)
    return gate * (1.0 + values * (1.0 - gate))


def layer_norm(values):
    center = values - jnp.mean(values, axis=-1, keepdims=True)
    inverse = lax.rsqrt(jnp.mean(center * center, axis=-1, keepdims=True) + EPSILON)
    return center * inverse, inverse


def dot(a, b, contract=(1, 0)):
    return lax.dot_general(
        a, b, (((contract[0],), (contract[1],)), ((), ())), preferred_element_type=F32
    )


def flip(index, bit):
    return index + bit * (1 - 2 * ((index // bit) % 2))


def flip_all(index, delta):
    bit = 1
    while bit <= delta:
        if delta & bit:
            index = flip(index, bit)
        bit *= 2
    return index


def plan_of(users, seqs, chunks):
    bits = []
    for axis, size in (("seq", seqs), ("users", users)):
        bit = 1
        while bit < size:
            bits.append((axis, bit))
            bit *= 2
    head, rest = bits[:1], bits[1:]
    turn, tail = rest[:3], rest[3:]
    devices = users * seqs
    each = -(-chunks // devices)
    streams = []
    base = 0
    for i in range(3):
        share = (each + 2 - i) // 3
        if share == 0:
            continue
        order = head + turn[i:] + turn[:i] + tail
        streams.append((base, share * devices, order))
        base += share * devices
    return streams, len(bits), base


def kernel(
    users,
    seqs,
    raw_ref,
    user_ref,
    place_ref,
    counts_ref,
    length_ref,
    cot_ref,
    enc_in_ref,
    enc_out_ref,
    proj_w_ref,
    proj_b_ref,
    out_w_ref,
    out_b_ref,
    layer_ref,
    gpw_ref,
    gpb_ref,
    gow_ref,
    gob_ref,
    send_buf,
    recv_buf,
    seq_sc,
    norm_sc,
    proj_sc,
    gate_sc,
    kv,
    qb,
    gb,
    w_sc,
    s_sc,
    att,
    dq,
    dk,
    dv,
    dproj,
    work,
    landing,
    full,
    bias,
    bias_in,
    a2a_send,
    a2a_recv,
    kv_send,
    kv_recv,
    q_send,
    q_recv,
    g_send,
    g_recv,
    rs_send,
    rs_recv,
    ag_send,
    ag_recv,
    b_send,
    b_recv,
):
    me_u = lax.axis_index("users")
    me_s = lax.axis_index("seq")
    MESH = pl.DeviceIdType.MESH
    slots, model = raw_ref.shape
    block = cot_ref.shape[0]
    width = out_w_ref.shape[0]
    pairs = width // LANES
    capacity = slots // users
    cap_pad = send_buf.shape[1]
    scale = HEAD ** (-0.5)

    barrier = pltpu.get_barrier_semaphore()
    for delta in range(1, users):
        pl.semaphore_signal(
            barrier,
            inc=1,
            device_id=(lax.rem(me_u + delta, users), me_s),
            device_id_type=MESH,
        )
    for delta in range(1, seqs):
        pl.semaphore_signal(
            barrier,
            inc=1,
            device_id=(me_u, lax.rem(me_s + delta, seqs)),
            device_id_type=MESH,
        )

    hidden = silu(dot(raw_ref[...], enc_in_ref[...])).astype(BF16)
    encoded = dot(hidden, enc_out_ref[...]).astype(BF16)
    target = user_ref[...]
    lane_row = lax.broadcasted_iota(jnp.int32, (1, slots), 1)
    first = jnp.zeros((1, slots), jnp.int32)
    total = jnp.int32(0)
    for u in range(users):
        first = jnp.where(target == u, total, first)
        total = total + counts_ref[0, u]
    flat = jnp.where(lane_row < total, target * cap_pad + lane_row - first, -1)
    hot = lax.broadcasted_iota(jnp.int32, (users * cap_pad, slots), 0) == flat
    bucket = dot(hot.astype(F32).astype(BF16), encoded).astype(BF16)
    local_place = (place_ref[...] - me_s * block + 1).astype(F32)
    spots = jnp.sum(jnp.where(hot, local_place, 0.0), axis=1, keepdims=True) - 1.0
    spots = jnp.broadcast_to(spots, (users * cap_pad, LANES)).astype(BF16)
    send_buf[:, :, :model] = bucket.reshape(users, cap_pad, model)
    send_buf[:, :, model:] = spots.reshape(users, cap_pad, LANES)

    pl.semaphore_wait(barrier, users - 1 + seqs - 1)

    sends = []
    for delta in range(1, users):
        peer = lax.rem(me_u + delta, users)
        copy = pltpu.make_async_remote_copy(
            src_ref=send_buf.at[peer],
            dst_ref=recv_buf.at[me_u],
            send_sem=a2a_send.at[delta],
            recv_sem=a2a_recv.at[delta],
            device_id=(peer, me_s),
            device_id_type=MESH,
        )
        copy.start()
        sends.append(copy)
    recv_buf[me_u] = send_buf[me_u]
    length = length_ref[0]
    rows = lax.broadcasted_iota(jnp.int32, (block, 1), 0)
    present = me_s * block + rows < length
    d_out = jnp.where(present, cot_ref[...], jnp.zeros((block, model), BF16))
    for copy in sends:
        copy.wait()
    arrived = recv_buf[...].reshape(users * cap_pad, model + LANES)
    where_to = arrived[:, model : model + 1].astype(F32).astype(jnp.int32)
    placed = (
        lax.broadcasted_iota(jnp.int32, (users * cap_pad, block), 1) == where_to
    ).astype(F32).astype(BF16)
    sequence = dot(placed, arrived[:, :model], (0, 0))
    seq_sc[...] = sequence.astype(BF16)
    normed = layer_norm(sequence)[0].astype(BF16)
    norm_sc[...] = normed
    projected = dot(normed, proj_w_ref[...]) + proj_b_ref[...]
    proj_sc[...] = projected
    gates = silu(projected).astype(BF16)
    gate_sc[...] = gates[:, :width]
    for p in range(pairs):
        low = p * LANES
        kv[me_s, p] = gates[:, 3 * width + low : 3 * width + low + LANES]
        kv[me_s, pairs + p] = gates[:, width + low : width + low + LANES]
        qb[me_s, p] = gates[:, 2 * width + low : 2 * width + low + LANES]

    steps = []
    bit = seqs // 2
    while bit >= 1:
        steps.append(bit)
        bit //= 2
    moves = []
    held = [0]
    for bit in steps:
        for delta in held:
            moves.append((delta, bit))
        held = held + [delta + bit for delta in held]

    def move(buf, send_sem, recv_sem, index):
        delta, bit = moves[index]
        held_block = flip_all(me_s, delta)
        peer = flip(me_s, bit)
        return (
            held_block,
            peer,
            pltpu.make_async_remote_copy(
                src_ref=buf.at[held_block],
                dst_ref=buf.at[held_block],
                send_sem=send_sem.at[index],
                recv_sem=recv_sem.at[delta + bit],
                device_id=(me_u, peer),
                device_id_type=MESH,
            ),
        )

    def arrive(buf, send_sem, recv_sem, delta):
        low_bit = delta & -delta
        source = flip_all(me_s, delta)
        pltpu.make_async_remote_copy(
            src_ref=buf.at[source],
            dst_ref=buf.at[source],
            send_sem=send_sem.at[0],
            recv_sem=recv_sem.at[delta],
            device_id=(me_u, flip(me_s, low_bit)),
            device_id_type=MESH,
        ).wait_recv()

    def up(held_block, peer):
        return held_block < peer

    def down(held_block, peer):
        return held_block > peer

    def start_own(buf, send_sem, recv_sem, way):
        for index, (delta, bit) in enumerate(moves):
            if delta == 0:
                held_block, peer, copy = move(buf, send_sem, recv_sem, index)

                @pl.when(way(held_block, peer))
                def _():
                    copy.start()

    def take(buf, send_sem, recv_sem, way, delta):
        source = flip_all(me_s, delta)

        @pl.when(way(source, me_s))
        def _():
            arrive(buf, send_sem, recv_sem, delta)
            for index, (held_delta, bit) in enumerate(moves):
                if held_delta == delta:
                    move(buf, send_sem, recv_sem, index)[2].start()

    def finish(buf, send_sem, recv_sem, way):
        for index in range(len(moves)):
            held_block, peer, copy = move(buf, send_sem, recv_sem, index)

            @pl.when(way(held_block, peer))
            def _():
                copy.wait_send()

    kv_set = (kv, kv_send, kv_recv, up)
    q_set = (qb, q_send, q_recv, down)
    g_set = (gb, g_send, g_recv, down)
    start_own(*kv_set)
    start_own(*q_set)

    lane_is_low = lax.broadcasted_iota(jnp.int32, (block, LANES), 1) < HEAD

    def half_of(values, hh):
        zero = jnp.zeros_like(values)
        return jnp.where(lane_is_low, values, zero) if hh == 0 else jnp.where(lane_is_low, zero, values)

    def scores_of(delta):
        other = flip_all(me_s, delta)
        q_index = jnp.maximum(other, me_s)
        k_index = jnp.minimum(other, me_s)
        bound = jnp.minimum(q_index * block + rows, length - 1) - k_index * block
        allowed = lax.broadcasted_iota(jnp.int32, (block, block), 1) <= bound
        for p in range(pairs):
            queries = qb[q_index, p]
            keys = kv[k_index, p]
            for hh in range(2):
                score = dot(half_of(queries, hh), keys, (1, 1)) * scale
                gate = sigmoid(score)
                plain = score * gate
                w_sc[delta, p, hh] = jnp.where(allowed, plain, 0.0).astype(BF16)
                s_sc[delta, p, hh] = jnp.where(allowed, gate + plain * (1.0 - gate), 0.0)

    def attend(delta):
        other = flip_all(me_s, delta)
        for p in range(pairs):
            values = kv[other, pairs + p]
            low = dot(w_sc[delta, p, 0], values)
            high = dot(w_sc[delta, p, 1], values)
            att[p] = att[p] + jnp.where(lane_is_low, low, high)

    att[...] = jnp.zeros_like(att)
    dq[...] = jnp.zeros_like(dq)
    dk[...] = jnp.zeros_like(dk)
    dv[...] = jnp.zeros_like(dv)
    scores_of(0)
    attend(0)
    order = sorted(range(1, seqs), key=lambda delta: (delta & -delta) * -1)
    for delta in order:
        take(*kv_set, delta)
        take(*q_set, delta)
    for delta in range(1, seqs):
        other = flip_all(me_s, delta)

        @pl.when(other < me_s)
        def _():
            scores_of(delta)
            attend(delta)

    attended = jnp.concatenate([att[p] for p in range(pairs)], axis=1)
    onorm, inverse = layer_norm(attended)
    gate_u = gate_sc[...].astype(F32)
    mixed = (onorm * gate_u).astype(BF16)
    d_mixed = dot(d_out, out_w_ref[...], (1, 1))
    d_gate_u = d_mixed * onorm
    d_onorm = d_mixed * gate_u
    d_att = (
        d_onorm
        - jnp.mean(d_onorm, axis=-1, keepdims=True)
        - onorm * jnp.mean(d_onorm * onorm, axis=-1, keepdims=True)
    ) * inverse
    d_att = d_att.astype(BF16)
    for p in range(pairs):
        gb[me_s, p] = d_att[:, p * LANES : (p + 1) * LANES]
    start_own(*g_set)
    projected_u = proj_sc[:, :width]
    dproj[:, :width] = (d_gate_u * silu_grad(projected_u)).astype(BF16)
    result = dot(mixed, out_w_ref[...]) + out_b_ref[...] + seq_sc[...].astype(F32)
    layer_ref[...] = jnp.where(present, result, 0.0).astype(BF16)
    bias[0] = jnp.zeros_like(bias[0])
    bias[0, 1:2, :model] = jnp.sum(d_out.astype(F32), axis=0, keepdims=True)
    grad_ow = dot(mixed, d_out, (0, 0)).astype(BF16)
    pw_chunks = model // ROWS
    ow_chunks = width // ROWS
    pw_tiles = 4 * width // LANES
    ow_tiles = model // LANES
    ow_base = pw_chunks * pw_tiles
    for tile in range(ow_tiles):
        work[ow_base + tile * ow_chunks : ow_base + (tile + 1) * ow_chunks] = grad_ow[
            :, tile * LANES : (tile + 1) * LANES
        ].reshape(ow_chunks, ROWS, LANES)
    used = ow_base + ow_tiles * ow_chunks
    if used < work.shape[0]:
        work[used:] = jnp.zeros((work.shape[0] - used, ROWS, LANES), BF16)

    for delta in range(1, seqs):
        other = flip_all(me_s, delta)

        @pl.when(other > me_s)
        def _():
            scores_of(delta)

    def backward(delta):
        other = flip_all(me_s, delta)
        q_index = jnp.maximum(other, me_s)
        k_index = jnp.minimum(other, me_s)
        for p in range(pairs):
            grads = gb[q_index, p]
            values = kv[k_index, pairs + p]
            d_scores = []
            for hh in range(2):
                d_weight = dot(half_of(grads, hh), values, (1, 1))
                d_scores.append((d_weight * s_sc[delta, p, hh]).astype(BF16))

            def query_side():
                keys = kv[k_index, p]
                dq[p] = dq[p] + jnp.where(
                    lane_is_low, dot(d_scores[0], keys), dot(d_scores[1], keys)
                )

            def key_side():
                queries = qb[q_index, p]
                dk[p] = dk[p] + jnp.where(
                    lane_is_low,
                    dot(d_scores[0], queries, (0, 0)),
                    dot(d_scores[1], queries, (0, 0)),
                )
                dv[p] = dv[p] + jnp.where(
                    lane_is_low,
                    dot(w_sc[delta, p, 0], grads, (0, 0)),
                    dot(w_sc[delta, p, 1], grads, (0, 0)),
                )

            if delta == 0:
                query_side()
                key_side()
            else:
                pl.when(other < me_s)(query_side)
                pl.when(other > me_s)(key_side)

    backward(0)
    for delta in range(1, seqs):
        other = flip_all(me_s, delta)

        @pl.when(other < me_s)
        def _():
            backward(delta)

    for delta in order:
        take(*g_set, delta)
    for delta in range(1, seqs):
        other = flip_all(me_s, delta)

        @pl.when(other > me_s)
        def _():
            backward(delta)

    for part, buf, factor in ((1, dv, 1.0), (2, dq, scale), (3, dk, scale)):
        slope = silu_grad(proj_sc[:, part * width : (part + 1) * width])
        for p in range(pairs):
            low = part * width + p * LANES
            dproj[:, low : low + LANES] = (
                buf[p] * factor * slope[:, p * LANES : (p + 1) * LANES]
            ).astype(BF16)

    d_proj = dproj[...]
    bias[0, 0:1, :] = jnp.sum(d_proj.astype(F32), axis=0, keepdims=True)
    grad_pw = dot(norm_sc[...], d_proj, (0, 0)).astype(BF16)
    for tile in range(pw_tiles):
        work[tile * pw_chunks : (tile + 1) * pw_chunks] = grad_pw[
            :, tile * LANES : (tile + 1) * LANES
        ].reshape(pw_chunks, ROWS, LANES)
    finish(*kv_set)
    finish(*q_set)
    finish(*g_set)

    streams, stages, _ = plan_of(users, seqs, used)

    def place_of(axis, bit):
        mine = me_s if axis == "seq" else me_u
        peer = flip(mine, bit)
        device = (me_u, peer) if axis == "seq" else (peer, me_s)
        return (mine // bit) % 2, device

    starts = [[base] for base, _, _ in streams]
    landing_at = 0
    for stage in range(stages):
        copies = []
        for i, (base, size, bit_order) in enumerate(streams):
            side, device = place_of(*bit_order[stage])
            half = size >> (stage + 1)
            start = starts[i][-1]
            copy = pltpu.make_async_remote_copy(
                src_ref=work.at[pl.ds(start + (1 - side) * half, half)],
                dst_ref=landing.at[pl.ds(landing_at, half)],
                send_sem=rs_send.at[stage, i],
                recv_sem=rs_recv.at[stage, i],
                device_id=device,
                device_id_type=MESH,
            )
            copy.start()
            copies.append((copy, start + side * half, half, landing_at))
            landing_at += half
        side, device = place_of(*streams[0][2][stage])
        bias_copy = pltpu.make_async_remote_copy(
            src_ref=bias.at[stage],
            dst_ref=bias_in.at[stage],
            send_sem=b_send.at[stage],
            recv_sem=b_recv.at[stage],
            device_id=device,
            device_id_type=MESH,
        )
        bias_copy.start()
        for i, (copy, keep, half, at) in enumerate(copies):
            copy.wait()
            work[pl.ds(keep, half)] = (
                work[pl.ds(keep, half)].astype(F32) + landing[at : at + half].astype(F32)
            ).astype(BF16)
            starts[i].append(keep)
        bias_copy.wait()
        bias[stage + 1] = bias[stage] + bias_in[stage]
    for i, (base, size, _) in enumerate(streams):
        share = size >> stages
        full[pl.ds(starts[i][-1], share)] = work[pl.ds(starts[i][-1], share)]
    for stage in range(stages - 1, -1, -1):
        copies = []
        for i, (base, size, bit_order) in enumerate(streams):
            _, device = place_of(*bit_order[stage])
            half = size >> (stage + 1)
            own = full.at[pl.ds(starts[i][stage + 1], half)]
            copy = pltpu.make_async_remote_copy(
                src_ref=own,
                dst_ref=own,
                send_sem=ag_send.at[stage, i],
                recv_sem=ag_recv.at[stage, i],
                device_id=device,
                device_id_type=MESH,
            )
            copy.start()
            copies.append(copy)
        for copy in copies:
            copy.wait()
    gpb_ref[...] = bias[stages, 0:1, :]
    gob_ref[...] = bias[stages, 1:2, :model]
    for tile in range(pw_tiles):
        gpw_ref[:, tile * LANES : (tile + 1) * LANES] = full[
            tile * pw_chunks : (tile + 1) * pw_chunks
        ].reshape(model, LANES)
    for tile in range(ow_tiles):
        gow_ref[:, tile * LANES : (tile + 1) * LANES] = full[
            ow_base + tile * ow_chunks : ow_base + (tile + 1) * ow_chunks
        ].reshape(width, LANES)


def on_device(
    users,
    seqs,
    raw_events,
    target_user,
    target_place,
    send_counts,
    lengths,
    cotangent,
    encoder_in,
    encoder_out,
    proj_weight,
    proj_bias,
    out_weight,
    out_bias,
):
    slots = raw_events.shape[1]
    block, model = cotangent.shape[1], cotangent.shape[2]
    width = out_weight.shape[0]
    pairs = width // LANES
    cap_pad = -(-(slots // users) // ROWS) * ROWS
    chunks = (model * 4 * width + width * model) // (ROWS * LANES)
    streams, stages, total = plan_of(users, seqs, chunks)
    count = len(streams)
    vmem = pl.BlockSpec(memory_space=pltpu.VMEM)
    smem = pl.BlockSpec(memory_space=pltpu.SMEM)
    dma = pltpu.SemaphoreType.DMA
    moves = seqs - 1
    result = pl.pallas_call(
        functools.partial(kernel, users, seqs),
        out_shape=(
            jax.ShapeDtypeStruct((block, model), BF16),
            jax.ShapeDtypeStruct((model, 4 * width), BF16),
            jax.ShapeDtypeStruct((1, 4 * width), F32),
            jax.ShapeDtypeStruct((width, model), BF16),
            jax.ShapeDtypeStruct((1, model), F32),
        ),
        in_specs=[vmem, vmem, vmem, smem, smem] + [vmem] * 7,
        out_specs=(vmem,) * 5,
        scratch_shapes=[
            pltpu.VMEM((users, cap_pad, model + LANES), BF16),
            pltpu.VMEM((users, cap_pad, model + LANES), BF16),
            pltpu.VMEM((block, model), BF16),
            pltpu.VMEM((block, model), BF16),
            pltpu.VMEM((block, 4 * width), F32),
            pltpu.VMEM((block, width), BF16),
            pltpu.VMEM((seqs, 2 * pairs, block, LANES), BF16),
            pltpu.VMEM((seqs, pairs, block, LANES), BF16),
            pltpu.VMEM((seqs, pairs, block, LANES), BF16),
            pltpu.VMEM((seqs, pairs, 2, block, block), BF16),
            pltpu.VMEM((seqs, pairs, 2, block, block), F32),
            pltpu.VMEM((pairs, block, LANES), F32),
            pltpu.VMEM((pairs, block, LANES), F32),
            pltpu.VMEM((pairs, block, LANES), F32),
            pltpu.VMEM((pairs, block, LANES), F32),
            pltpu.VMEM((block, 4 * width), BF16),
            pltpu.VMEM((total, ROWS, LANES), BF16),
            pltpu.VMEM((total, ROWS, LANES), BF16),
            pltpu.VMEM((total, ROWS, LANES), BF16),
            pltpu.VMEM((stages + 1, 2, 4 * width), F32),
            pltpu.VMEM((stages, 2, 4 * width), F32),
            dma((users,)),
            dma((users,)),
            dma((moves,)),
            dma((seqs,)),
            dma((moves,)),
            dma((seqs,)),
            dma((moves,)),
            dma((seqs,)),
            dma((stages, count)),
            dma((stages, count)),
            dma((stages, count)),
            dma((stages, count)),
            dma((stages,)),
            dma((stages,)),
        ],
        compiler_params=pltpu.CompilerParams(
            collective_id=0, has_side_effects=True, vmem_limit_bytes=60000 * 1024
        ),
    )(
        raw_events[0],
        target_user,
        target_place,
        send_counts[0],
        lengths,
        cotangent[0],
        encoder_in,
        encoder_out,
        proj_weight,
        proj_bias[None],
        out_weight,
        out_bias[None],
    )
    layer_out, grad_pw, grad_pb, grad_ow, grad_ob = result
    return layer_out[None], grad_pw, grad_pb[0], grad_ow, grad_ob[0]


def solution(mesh):
    placed = (
        P("seq", "users", None),
        P("seq", "users"),
        P("seq", "users"),
        P("seq", "users", None),
        P("users"),
        P("users", "seq", None),
        P(),
        P(),
        P(),
        P(),
        P(),
        P(),
    )
    return jax.shard_map(
        functools.partial(on_device, mesh.shape["users"], mesh.shape["seq"]),
        mesh=mesh,
        in_specs=placed,
        out_specs=(P("users", "seq", None), P(), P(), P(), P()),
        check_vma=False,
    )
```

```python
import functools

import jax
import jax.numpy as jnp
from jax import lax
from jax.experimental import pallas as pl
from jax.experimental.pallas import tpu as pltpu
from jax.sharding import PartitionSpec as P

HEAD = 64
EPSILON = 1e-05
LANES = 128
ROWS = 16
F32 = jnp.float32
BF16 = jnp.bfloat16


def sigmoid(values):
    return 0.5 * jnp.tanh(0.5 * values) + 0.5


def silu(values):
    return values * sigmoid(values)


def silu_grad(values):
    gate = sigmoid(values)
    return gate * (1.0 + values * (1.0 - gate))


def layer_norm(values):
    center = values - jnp.mean(values, axis=-1, keepdims=True)
    inverse = lax.rsqrt(jnp.mean(center * center, axis=-1, keepdims=True) + EPSILON)
    return center * inverse, inverse


def dot(a, b, contract=(1, 0)):
    return lax.dot_general(
        a, b, (((contract[0],), (contract[1],)), ((), ())), preferred_element_type=F32
    )


def flip(index, bit):
    return index + bit * (1 - 2 * ((index // bit) % 2))


def flip_all(index, delta):
    bit = 1
    while bit <= delta:
        if delta & bit:
            index = flip(index, bit)
        bit *= 2
    return index


def plan_of(users, seqs, groups):
    bits = []
    for axis, size in (("seq", seqs), ("users", users)):
        bit = 1
        while bit < size:
            bits.append((axis, bit))
            bit *= 2
    head, rest = bits[:1], bits[1:]
    turn, tail = rest[:3], rest[3:]
    devices = users * seqs
    plans = []
    base = 0
    for chunks, most in groups:
        each = -(-chunks // devices)
        streams = []
        for i in range(most):
            share = (each + most - 1 - i) // most
            if share == 0:
                continue
            k = i % 3
            order = head + turn[k:] + turn[:k] + tail
            streams.append((base, share * devices, order))
            base += share * devices
        plans.append(streams)
    return plans, len(bits), base


def groups_of(model, width):
    tile = ROWS * LANES
    return (2 * model * width // tile, 3), (3 * model * width // tile, 6)


def kernel(
    users,
    seqs,
    raw_ref,
    user_ref,
    place_ref,
    counts_ref,
    length_ref,
    cot_ref,
    enc_in_ref,
    enc_out_ref,
    proj_w_ref,
    proj_b_ref,
    out_w_ref,
    out_b_ref,
    layer_ref,
    full,
    bias_ref,
    send_buf,
    recv_buf,
    spot_out,
    spot_in,
    seq_sc,
    norm_sc,
    proj_sc,
    gate_sc,
    kv,
    qb,
    gb,
    w_sc,
    s_sc,
    att,
    dq,
    dk,
    dv,
    dproj,
    work,
    landing,
    bias,
    bias_in,
    a2a_send,
    a2a_recv,
    spot_send,
    spot_recv,
    kv_send,
    kv_recv,
    q_send,
    q_recv,
    g_send,
    g_recv,
    rs_send,
    rs_recv,
    ag_send,
    ag_recv,
    b_send,
    b_recv,
):
    me_u = lax.axis_index("users")
    me_s = lax.axis_index("seq")
    MESH = pl.DeviceIdType.MESH
    slots, model = raw_ref.shape
    block = cot_ref.shape[0]
    width = out_w_ref.shape[0]
    pairs = width // LANES
    capacity = slots // users
    cap_pad = send_buf.shape[1]
    scale = HEAD ** (-0.5)

    barrier = pltpu.get_barrier_semaphore()
    for delta in range(1, users):
        pl.semaphore_signal(
            barrier,
            inc=1,
            device_id=(lax.rem(me_u + delta, users), me_s),
            device_id_type=MESH,
        )
    for delta in range(1, seqs):
        pl.semaphore_signal(
            barrier,
            inc=1,
            device_id=(me_u, lax.rem(me_s + delta, seqs)),
            device_id_type=MESH,
        )

    hidden = silu(dot(raw_ref[...], enc_in_ref[...])).astype(BF16)
    encoded = dot(hidden, enc_out_ref[...]).astype(BF16)
    target = user_ref[...]
    lane_row = lax.broadcasted_iota(jnp.int32, (1, slots), 1)
    first = jnp.zeros((1, slots), jnp.int32)
    total = jnp.int32(0)
    for u in range(users):
        first = jnp.where(target == u, total, first)
        total = total + counts_ref[0, u]
    flat = jnp.where(lane_row < total, target * cap_pad + lane_row - first, -1)
    hot = lax.broadcasted_iota(jnp.int32, (users * cap_pad, slots), 0) == flat
    bucket = dot(hot.astype(F32).astype(BF16), encoded).astype(BF16)
    local_place = (place_ref[...] - me_s * block + 1).astype(F32)
    spots = jnp.sum(jnp.where(hot, local_place, 0.0), axis=1, keepdims=True) - 1.0
    diagonal = lax.broadcasted_iota(
        jnp.int32, (users, cap_pad, LANES), 1
    ) == lax.broadcasted_iota(jnp.int32, (users, cap_pad, LANES), 2)
    send_buf[...] = bucket.reshape(users, cap_pad, model)
    spot_out[...] = jnp.sum(
        jnp.where(diagonal, spots.reshape(users, cap_pad, 1), 0.0), axis=1, keepdims=True
    )

    pl.semaphore_wait(barrier, users - 1 + seqs - 1)

    sends = []
    for delta in range(1, users):
        peer = lax.rem(me_u + delta, users)
        copy = pltpu.make_async_remote_copy(
            src_ref=send_buf.at[peer],
            dst_ref=recv_buf.at[me_u],
            send_sem=a2a_send.at[delta],
            recv_sem=a2a_recv.at[delta],
            device_id=(peer, me_s),
            device_id_type=MESH,
        )
        spot_copy = pltpu.make_async_remote_copy(
            src_ref=spot_out.at[peer],
            dst_ref=spot_in.at[me_u],
            send_sem=spot_send.at[delta],
            recv_sem=spot_recv.at[delta],
            device_id=(peer, me_s),
            device_id_type=MESH,
        )
        spot_copy.start()
        copy.start()
        sends.append(spot_copy)
        sends.append(copy)
    recv_buf[me_u] = send_buf[me_u]
    spot_in[me_u] = spot_out[me_u]
    length = length_ref[0]
    rows = lax.broadcasted_iota(jnp.int32, (block, 1), 0)
    present = me_s * block + rows < length
    d_out = jnp.where(present, cot_ref[...], jnp.zeros((block, model), BF16))
    for copy in sends:
        copy.wait()
    arrived = recv_buf[...].reshape(users * cap_pad, model)
    where_to = jnp.sum(jnp.where(diagonal, spot_in[...], 0.0), axis=2, keepdims=True)
    where_to = where_to.reshape(users * cap_pad, 1).astype(jnp.int32)
    placed = (
        lax.broadcasted_iota(jnp.int32, (users * cap_pad, block), 1) == where_to
    ).astype(F32).astype(BF16)
    sequence = dot(placed, arrived, (0, 0))
    seq_sc[...] = sequence.astype(BF16)
    normed = layer_norm(sequence)[0].astype(BF16)
    norm_sc[...] = normed
    projected = dot(normed, proj_w_ref[...]) + proj_b_ref[...]
    proj_sc[...] = projected
    gates = silu(projected).astype(BF16)
    gate_sc[...] = gates[:, :width]
    for p in range(pairs):
        low = p * LANES
        kv[me_s, p] = gates[:, 3 * width + low : 3 * width + low + LANES]
        kv[me_s, pairs + p] = gates[:, width + low : width + low + LANES]
        qb[me_s, p] = gates[:, 2 * width + low : 2 * width + low + LANES]

    steps = []
    bit = seqs // 2
    while bit >= 1:
        steps.append(bit)
        bit //= 2
    moves = []
    held = [0]
    for bit in steps:
        for delta in held:
            moves.append((delta, bit))
        held = held + [delta + bit for delta in held]

    def move(buf, send_sem, recv_sem, index):
        delta, bit = moves[index]
        held_block = flip_all(me_s, delta)
        peer = flip(me_s, bit)
        return (
            held_block,
            peer,
            pltpu.make_async_remote_copy(
                src_ref=buf.at[held_block],
                dst_ref=buf.at[held_block],
                send_sem=send_sem.at[index],
                recv_sem=recv_sem.at[delta + bit],
                device_id=(me_u, peer),
                device_id_type=MESH,
            ),
        )

    def arrive(buf, send_sem, recv_sem, delta):
        low_bit = delta & -delta
        source = flip_all(me_s, delta)
        pltpu.make_async_remote_copy(
            src_ref=buf.at[source],
            dst_ref=buf.at[source],
            send_sem=send_sem.at[0],
            recv_sem=recv_sem.at[delta],
            device_id=(me_u, flip(me_s, low_bit)),
            device_id_type=MESH,
        ).wait_recv()

    def up(held_block, peer):
        return held_block < peer

    def down(held_block, peer):
        return held_block > peer

    def start_own(buf, send_sem, recv_sem, way):
        for index, (delta, bit) in enumerate(moves):
            if delta == 0:
                held_block, peer, copy = move(buf, send_sem, recv_sem, index)

                @pl.when(way(held_block, peer))
                def _():
                    copy.start()

    def take(buf, send_sem, recv_sem, way, delta):
        source = flip_all(me_s, delta)

        @pl.when(way(source, me_s))
        def _():
            arrive(buf, send_sem, recv_sem, delta)
            for index, (held_delta, bit) in enumerate(moves):
                if held_delta == delta:
                    move(buf, send_sem, recv_sem, index)[2].start()

    def finish(buf, send_sem, recv_sem, way):
        for index in range(len(moves)):
            held_block, peer, copy = move(buf, send_sem, recv_sem, index)

            @pl.when(way(held_block, peer))
            def _():
                copy.wait_send()

    kv_set = (kv, kv_send, kv_recv, up)
    q_set = (qb, q_send, q_recv, down)
    g_set = (gb, g_send, g_recv, down)
    start_own(*kv_set)
    start_own(*q_set)

    lane_is_low = lax.broadcasted_iota(jnp.int32, (block, LANES), 1) < HEAD

    def half_of(values, hh):
        zero = jnp.zeros_like(values)
        return jnp.where(lane_is_low, values, zero) if hh == 0 else jnp.where(lane_is_low, zero, values)

    def scores_of(delta):
        other = flip_all(me_s, delta)
        q_index = jnp.maximum(other, me_s)
        k_index = jnp.minimum(other, me_s)
        bound = jnp.minimum(q_index * block + rows, length - 1) - k_index * block
        allowed = lax.broadcasted_iota(jnp.int32, (block, block), 1) <= bound
        for p in range(pairs):
            queries = qb[q_index, p]
            keys = kv[k_index, p]
            for hh in range(2):
                score = dot(half_of(queries, hh), keys, (1, 1)) * scale
                gate = sigmoid(score)
                plain = score * gate
                w_sc[delta, p, hh] = jnp.where(allowed, plain, 0.0).astype(BF16)
                s_sc[delta, p, hh] = jnp.where(allowed, gate + plain * (1.0 - gate), 0.0)

    def attend(delta):
        other = flip_all(me_s, delta)
        for p in range(pairs):
            values = kv[other, pairs + p]
            low = dot(w_sc[delta, p, 0], values)
            high = dot(w_sc[delta, p, 1], values)
            att[p] = att[p] + jnp.where(lane_is_low, low, high)

    att[...] = jnp.zeros_like(att)
    dq[...] = jnp.zeros_like(dq)
    dk[...] = jnp.zeros_like(dk)
    dv[...] = jnp.zeros_like(dv)
    scores_of(0)
    attend(0)
    for delta in range(1, seqs):
        other = flip_all(me_s, delta)
        take(*kv_set, delta)
        take(*q_set, delta)

        @pl.when(other < me_s)
        def _():
            scores_of(delta)
            attend(delta)

    attended = jnp.concatenate([att[p] for p in range(pairs)], axis=1)
    onorm, inverse = layer_norm(attended)
    gate_u = gate_sc[...].astype(F32)
    mixed = (onorm * gate_u).astype(BF16)
    d_mixed = dot(d_out, out_w_ref[...], (1, 1))
    d_gate_u = d_mixed * onorm
    d_onorm = d_mixed * gate_u
    d_att = (
        d_onorm
        - jnp.mean(d_onorm, axis=-1, keepdims=True)
        - onorm * jnp.mean(d_onorm * onorm, axis=-1, keepdims=True)
    ) * inverse
    d_att = d_att.astype(BF16)
    for p in range(pairs):
        gb[me_s, p] = d_att[:, p * LANES : (p + 1) * LANES]
    start_own(*g_set)
    projected_u = proj_sc[:, :width]
    dproj[:, :width] = (d_gate_u * silu_grad(projected_u)).astype(BF16)
    result = dot(mixed, out_w_ref[...]) + out_b_ref[...] + seq_sc[...].astype(F32)
    layer_ref[...] = jnp.where(present, result, 0.0).astype(BF16)
    bias[0] = jnp.zeros_like(bias[0])
    bias[0, 1:2, :model] = jnp.sum(d_out.astype(F32), axis=0, keepdims=True)
    (early, late), stages, total_chunks = plan_of(users, seqs, groups_of(model, width))
    late_base = late[0][0]

    def store_tiles(base, values):
        height = values.shape[0] // ROWS
        for tile in range(values.shape[1] // LANES):
            work[base + tile * height : base + (tile + 1) * height] = values[
                :, tile * LANES : (tile + 1) * LANES
            ].reshape(height, ROWS, LANES)
        return base + values.shape[0] * values.shape[1] // (ROWS * LANES)

    def clear(base, stop):
        if base < stop:
            work[base:stop] = jnp.zeros((stop - base, ROWS, LANES), BF16)

    filled = store_tiles(0, dot(mixed, d_out, (0, 0)).astype(BF16))
    filled = store_tiles(filled, dot(norm_sc[...], dproj[:, :width], (0, 0)).astype(BF16))
    clear(filled, late_base)

    def place_of(axis, bit):
        mine = me_s if axis == "seq" else me_u
        peer = flip(mine, bit)
        device = (me_u, peer) if axis == "seq" else (peer, me_s)
        return (mine // bit) % 2, device

    all_streams = early + late
    starts = [[base] for base, _, _ in all_streams]
    landings = []
    landing_at = 0
    for base, size, _ in all_streams:
        offsets = []
        for stage in range(stages):
            offsets.append(landing_at)
            landing_at += size >> (stage + 1)
        landings.append(offsets)
    early_ids = list(range(len(early)))
    late_ids = list(range(len(early), len(all_streams)))

    def reduce_copy(i, stage):
        base, size, bit_order = all_streams[i]
        side, device = place_of(*bit_order[stage])
        half = size >> (stage + 1)
        start = starts[i][stage]
        return (
            pltpu.make_async_remote_copy(
                src_ref=work.at[pl.ds(start + (1 - side) * half, half)],
                dst_ref=landing.at[pl.ds(landings[i][stage], half)],
                send_sem=rs_send.at[i, stage],
                recv_sem=rs_recv.at[i, stage],
                device_id=device,
                device_id_type=MESH,
            ),
            start + side * half,
            half,
        )

    def gather_copy(i, stage):
        base, size, bit_order = all_streams[i]
        _, device = place_of(*bit_order[stage])
        half = size >> (stage + 1)
        own = full.at[pl.ds(starts[i][stage + 1], half)]
        return pltpu.make_async_remote_copy(
            src_ref=own,
            dst_ref=own,
            send_sem=ag_send.at[i, stage],
            recv_sem=ag_recv.at[i, stage],
            device_id=device,
            device_id_type=MESH,
        )

    def reduce_start(ids):
        for i in ids:
            reduce_copy(i, 0)[0].start()

    def reduce_step(ids, stage):
        for i in ids:
            copy, keep, half = reduce_copy(i, stage)
            copy.wait()
            at = landings[i][stage]
            summed = (
                work[pl.ds(keep, half)].astype(F32) + landing[at : at + half].astype(F32)
            ).astype(BF16)
            starts[i].append(keep)
            if stage + 1 < stages:
                work[pl.ds(keep, half)] = summed
                reduce_copy(i, stage + 1)[0].start()
            else:
                full[pl.ds(keep, half)] = summed
                gather_copy(i, stage).start()

    def gather_step(ids, stage):
        for i in ids:
            gather_copy(i, stage).wait()
            if stage > 0:
                gather_copy(i, stage - 1).start()

    reduce_start(early_ids)

    for delta in range(1, seqs):
        other = flip_all(me_s, delta)

        @pl.when(other > me_s)
        def _():
            scores_of(delta)

    reduce_step(early_ids, 0)

    def backward(delta):
        other = flip_all(me_s, delta)
        q_index = jnp.maximum(other, me_s)
        k_index = jnp.minimum(other, me_s)
        for p in range(pairs):
            grads = gb[q_index, p]
            values = kv[k_index, pairs + p]
            d_scores = []
            for hh in range(2):
                d_weight = dot(half_of(grads, hh), values, (1, 1))
                d_scores.append((d_weight * s_sc[delta, p, hh]).astype(BF16))

            def query_side():
                keys = kv[k_index, p]
                dq[p] = dq[p] + jnp.where(
                    lane_is_low, dot(d_scores[0], keys), dot(d_scores[1], keys)
                )

            def key_side():
                queries = qb[q_index, p]
                dk[p] = dk[p] + jnp.where(
                    lane_is_low,
                    dot(d_scores[0], queries, (0, 0)),
                    dot(d_scores[1], queries, (0, 0)),
                )
                dv[p] = dv[p] + jnp.where(
                    lane_is_low,
                    dot(w_sc[delta, p, 0], grads, (0, 0)),
                    dot(w_sc[delta, p, 1], grads, (0, 0)),
                )

            if delta == 0:
                query_side()
                key_side()
            else:
                pl.when(other < me_s)(query_side)
                pl.when(other > me_s)(key_side)

    backward(0)
    reduce_step(early_ids, 1)
    for delta in range(1, seqs):
        other = flip_all(me_s, delta)

        @pl.when(other < me_s)
        def _():
            backward(delta)

    reduce_step(early_ids, 2)
    early_done = 3
    for delta in range(1, seqs):
        other = flip_all(me_s, delta)
        take(*g_set, delta)

        @pl.when(other > me_s)
        def _():
            backward(delta)

    for part, buf, factor in ((1, dv, 1.0), (2, dq, scale), (3, dk, scale)):
        slope = silu_grad(proj_sc[:, part * width : (part + 1) * width])
        for p in range(pairs):
            low = part * width + p * LANES
            dproj[:, low : low + LANES] = (
                buf[p] * factor * slope[:, p * LANES : (p + 1) * LANES]
            ).astype(BF16)

    d_proj = dproj[...]
    filled = store_tiles(late_base, dot(norm_sc[...], d_proj[:, width:], (0, 0)).astype(BF16))
    clear(filled, total_chunks)
    reduce_start(late_ids)
    bias[0, 0:1, :] = jnp.sum(d_proj.astype(F32), axis=0, keepdims=True)

    def bias_copy(stage):
        _, device = place_of(*all_streams[0][2][stage])
        return pltpu.make_async_remote_copy(
            src_ref=bias.at[stage],
            dst_ref=bias_in.at[stage],
            send_sem=b_send.at[stage],
            recv_sem=b_recv.at[stage],
            device_id=device,
            device_id_type=MESH,
        )

    def bias_step(stage):
        bias_copy(stage).wait()
        bias[stage + 1] = bias[stage] + bias_in[stage]
        if stage + 1 < stages:
            bias_copy(stage + 1).start()

    bias_copy(0).start()
    for stage in range(early_done, stages):
        reduce_step(early_ids, stage)
    for stage in range(stages):
        reduce_step(late_ids, stage)
        gather_step(early_ids, stages - 1 - stage)
        bias_step(stage)
    for stage in range(stages - 1, -1, -1):
        gather_step(late_ids, stage)
    bias_ref[...] = bias[stages]
    finish(*kv_set)
    finish(*q_set)
    finish(*g_set)


def unpack(full, bias_ref, layer_in, layer_ref, gpw_ref, gpb_ref, gow_ref, gob_ref, late_base):
    model, width = gow_ref.shape[1], gow_ref.shape[0]
    layer_ref[...] = layer_in[...]
    gpb_ref[...] = bias_ref[0:1, :]
    gob_ref[...] = bias_ref[1:2, :model]

    def tile_of(base, height):
        return full[base : base + height // ROWS].reshape(height, LANES)

    at = 0
    for tile in range(model // LANES):
        gow_ref[:, tile * LANES : (tile + 1) * LANES] = tile_of(at, width)
        at += width // ROWS
    for tile in range(4 * width // LANES):
        if tile == width // LANES:
            at = late_base
        gpw_ref[:, tile * LANES : (tile + 1) * LANES] = tile_of(at, model)
        at += model // ROWS


def on_device(
    users,
    seqs,
    raw_events,
    target_user,
    target_place,
    send_counts,
    lengths,
    cotangent,
    encoder_in,
    encoder_out,
    proj_weight,
    proj_bias,
    out_weight,
    out_bias,
):
    slots = raw_events.shape[1]
    block, model = cotangent.shape[1], cotangent.shape[2]
    width = out_weight.shape[0]
    pairs = width // LANES
    cap_pad = -(-(slots // users) // ROWS) * ROWS
    (early, late), stages, total = plan_of(users, seqs, groups_of(model, width))
    count = len(early) + len(late)
    vmem = pl.BlockSpec(memory_space=pltpu.VMEM)
    smem = pl.BlockSpec(memory_space=pltpu.SMEM)
    dma = pltpu.SemaphoreType.DMA
    moves = seqs - 1
    layer, full, bias = pl.pallas_call(
        functools.partial(kernel, users, seqs),
        out_shape=(
            jax.ShapeDtypeStruct((block, model), BF16),
            jax.ShapeDtypeStruct((total, ROWS, LANES), BF16),
            jax.ShapeDtypeStruct((2, 4 * width), F32),
        ),
        in_specs=[vmem, vmem, vmem, smem, smem] + [vmem] * 7,
        out_specs=(vmem,) * 3,
        scratch_shapes=[
            pltpu.VMEM((users, cap_pad, model), BF16),
            pltpu.VMEM((users, cap_pad, model), BF16),
            pltpu.VMEM((users, 1, LANES), F32),
            pltpu.VMEM((users, 1, LANES), F32),
            pltpu.VMEM((block, model), BF16),
            pltpu.VMEM((block, model), BF16),
            pltpu.VMEM((block, 4 * width), F32),
            pltpu.VMEM((block, width), BF16),
            pltpu.VMEM((seqs, 2 * pairs, block, LANES), BF16),
            pltpu.VMEM((seqs, pairs, block, LANES), BF16),
            pltpu.VMEM((seqs, pairs, block, LANES), BF16),
            pltpu.VMEM((seqs, pairs, 2, block, block), BF16),
            pltpu.VMEM((seqs, pairs, 2, block, block), F32),
            pltpu.VMEM((pairs, block, LANES), F32),
            pltpu.VMEM((pairs, block, LANES), F32),
            pltpu.VMEM((pairs, block, LANES), F32),
            pltpu.VMEM((pairs, block, LANES), F32),
            pltpu.VMEM((block, 4 * width), BF16),
            pltpu.VMEM((total, ROWS, LANES), BF16),
            pltpu.VMEM((total, ROWS, LANES), BF16),
            pltpu.VMEM((stages + 1, 2, 4 * width), F32),
            pltpu.VMEM((stages, 2, 4 * width), F32),
            dma((users,)),
            dma((users,)),
            dma((users,)),
            dma((users,)),
            dma((moves,)),
            dma((seqs,)),
            dma((moves,)),
            dma((seqs,)),
            dma((moves,)),
            dma((seqs,)),
            dma((count, stages)),
            dma((count, stages)),
            dma((count, stages)),
            dma((count, stages)),
            dma((stages,)),
            dma((stages,)),
        ],
        compiler_params=pltpu.CompilerParams(
            collective_id=0, has_side_effects=True, vmem_limit_bytes=60000 * 1024
        ),
    )(
        raw_events[0],
        target_user,
        target_place,
        send_counts[0],
        lengths,
        cotangent[0],
        encoder_in,
        encoder_out,
        proj_weight,
        proj_bias[None],
        out_weight,
        out_bias[None],
    )
    layer_out, grad_pw, grad_pb, grad_ow, grad_ob = pl.pallas_call(
        functools.partial(unpack, late_base=late[0][0]),
        out_shape=(
            jax.ShapeDtypeStruct((block, model), BF16),
            jax.ShapeDtypeStruct((model, 4 * width), BF16),
            jax.ShapeDtypeStruct((1, 4 * width), F32),
            jax.ShapeDtypeStruct((width, model), BF16),
            jax.ShapeDtypeStruct((1, model), F32),
        ),
        in_specs=[vmem] * 3,
        out_specs=(vmem,) * 5,
    )(full, bias, layer)
    return layer_out[None], grad_pw, grad_pb[0], grad_ow, grad_ob[0]


def solution(mesh):
    placed = (
        P("seq", "users", None),
        P("seq", "users"),
        P("seq", "users"),
        P("seq", "users", None),
        P("users"),
        P("users", "seq", None),
        P(),
        P(),
        P(),
        P(),
        P(),
        P(),
    )
    return jax.shard_map(
        functools.partial(on_device, mesh.shape["users"], mesh.shape["seq"]),
        mesh=mesh,
        in_specs=placed,
        out_specs=(P("users", "seq", None), P(), P(), P(), P()),
        check_vma=False,
    )
```

```python
import functools

import jax
import jax.numpy as jnp
from jax import lax
from jax.experimental import pallas as pl
from jax.experimental.pallas import tpu as pltpu
from jax.sharding import PartitionSpec as P

HEAD = 64
EPSILON = 1e-05
LANES = 128
ROWS = 16
F32 = jnp.float32
BF16 = jnp.bfloat16


def sigmoid(values):
    return 0.5 * jnp.tanh(0.5 * values) + 0.5


def silu(values):
    return values * sigmoid(values)


def silu_grad(values):
    gate = sigmoid(values)
    return gate * (1.0 + values * (1.0 - gate))


def layer_norm(values):
    center = values - jnp.mean(values, axis=-1, keepdims=True)
    inverse = lax.rsqrt(jnp.mean(center * center, axis=-1, keepdims=True) + EPSILON)
    return center * inverse, inverse


def dot(a, b, contract=(1, 0)):
    return lax.dot_general(
        a, b, (((contract[0],), (contract[1],)), ((), ())), preferred_element_type=F32
    )


def flip(index, bit):
    return index + bit * (1 - 2 * ((index // bit) % 2))


def flip_all(index, delta):
    bit = 1
    while bit <= delta:
        if delta & bit:
            index = flip(index, bit)
        bit *= 2
    return index


def plan_of(users, seqs, groups):
    bits = []
    for axis, size in (("seq", seqs), ("users", users)):
        bit = 1
        while bit < size:
            bits.append((axis, bit))
            bit *= 2
    head, rest = bits[:1], bits[1:]
    turn, tail = rest[:3], rest[3:]
    devices = users * seqs
    plans = []
    base = 0
    for chunks, most in groups:
        each = -(-chunks // devices)
        streams = []
        for i in range(most):
            share = (each + most - 1 - i) // most
            if share == 0:
                continue
            k = i % 3
            order = head + turn[k:] + turn[:k] + tail
            streams.append((base, share * devices, order))
            base += share * devices
        plans.append(streams)
    return plans, len(bits), base


def groups_of(model, width):
    tile = ROWS * LANES
    return (2 * model * width // tile, 3), (3 * model * width // tile, 6)


def kernel(
    users,
    seqs,
    raw_hbm,
    user_ref,
    place_ref,
    counts_ref,
    length_ref,
    cot_hbm,
    enc_in_hbm,
    enc_out_hbm,
    proj_w_hbm,
    proj_b_ref,
    out_w_hbm,
    out_b_ref,
    layer_ref,
    full,
    bias_ref,
    send_buf,
    recv_buf,
    spot_out,
    spot_in,
    seq_sc,
    norm_sc,
    proj_sc,
    gate_sc,
    kv,
    qb,
    gb,
    w_sc,
    s_sc,
    att,
    dq,
    dk,
    dv,
    dproj,
    work,
    landing,
    bias,
    bias_in,
    a2a_send,
    a2a_recv,
    spot_send,
    spot_recv,
    kv_send,
    kv_recv,
    q_send,
    q_recv,
    g_send,
    g_recv,
    rs_send,
    rs_recv,
    ag_send,
    ag_recv,
    b_send,
    b_recv,
    raw_ref,
    cot_ref,
    enc_in_ref,
    enc_out_ref,
    proj_w_ref,
    out_w_ref,
    in_sem,
):
    me_u = lax.axis_index("users")
    me_s = lax.axis_index("seq")
    MESH = pl.DeviceIdType.MESH
    slots, model = raw_ref.shape
    block = cot_ref.shape[0]
    width = out_w_ref.shape[0]
    pairs = width // LANES
    capacity = slots // users
    cap_pad = send_buf.shape[1]
    scale = HEAD ** (-0.5)

    barrier = pltpu.get_barrier_semaphore()
    for delta in range(1, users):
        pl.semaphore_signal(
            barrier,
            inc=1,
            device_id=(lax.rem(me_u + delta, users), me_s),
            device_id_type=MESH,
        )
    for delta in range(1, seqs):
        pl.semaphore_signal(
            barrier,
            inc=1,
            device_id=(me_u, lax.rem(me_s + delta, seqs)),
            device_id_type=MESH,
        )

    loads = [
        pltpu.make_async_copy(source, target, in_sem.at[i])
        for i, (source, target) in enumerate(
            (
                (raw_hbm, raw_ref),
                (enc_in_hbm, enc_in_ref),
                (enc_out_hbm, enc_out_ref),
                (cot_hbm, cot_ref),
                (proj_w_hbm, proj_w_ref),
                (out_w_hbm, out_w_ref),
            )
        )
    ]
    for load in loads:
        load.start()

    loads[0].wait()
    loads[1].wait()
    loads[2].wait()
    hidden = silu(dot(raw_ref[...], enc_in_ref[...])).astype(BF16)
    encoded = dot(hidden, enc_out_ref[...]).astype(BF16)
    target = user_ref[...]
    lane_row = lax.broadcasted_iota(jnp.int32, (1, slots), 1)
    first = jnp.zeros((1, slots), jnp.int32)
    total = jnp.int32(0)
    for u in range(users):
        first = jnp.where(target == u, total, first)
        total = total + counts_ref[0, u]
    flat = jnp.where(lane_row < total, target * cap_pad + lane_row - first, -1)
    hot = lax.broadcasted_iota(jnp.int32, (users * cap_pad, slots), 0) == flat
    bucket = dot(hot.astype(F32).astype(BF16), encoded).astype(BF16)
    local_place = (place_ref[...] - me_s * block + 1).astype(F32)
    spots = jnp.sum(jnp.where(hot, local_place, 0.0), axis=1, keepdims=True) - 1.0
    diagonal = lax.broadcasted_iota(
        jnp.int32, (users, cap_pad, LANES), 1
    ) == lax.broadcasted_iota(jnp.int32, (users, cap_pad, LANES), 2)
    send_buf[...] = bucket.reshape(users, cap_pad, model)
    spot_out[...] = jnp.sum(
        jnp.where(diagonal, spots.reshape(users, cap_pad, 1), 0.0), axis=1, keepdims=True
    )

    pl.semaphore_wait(barrier, users - 1 + seqs - 1)

    sends = []
    for delta in range(1, users):
        peer = lax.rem(me_u + delta, users)
        copy = pltpu.make_async_remote_copy(
            src_ref=send_buf.at[peer],
            dst_ref=recv_buf.at[me_u],
            send_sem=a2a_send.at[delta],
            recv_sem=a2a_recv.at[delta],
            device_id=(peer, me_s),
            device_id_type=MESH,
        )
        spot_copy = pltpu.make_async_remote_copy(
            src_ref=spot_out.at[peer],
            dst_ref=spot_in.at[me_u],
            send_sem=spot_send.at[delta],
            recv_sem=spot_recv.at[delta],
            device_id=(peer, me_s),
            device_id_type=MESH,
        )
        spot_copy.start()
        copy.start()
        sends.append(spot_copy)
        sends.append(copy)
    recv_buf[me_u] = send_buf[me_u]
    spot_in[me_u] = spot_out[me_u]
    length = length_ref[0]
    rows = lax.broadcasted_iota(jnp.int32, (block, 1), 0)
    present = me_s * block + rows < length
    loads[3].wait()
    loads[4].wait()
    loads[5].wait()
    d_out = jnp.where(present, cot_ref[...], jnp.zeros((block, model), BF16))
    for copy in sends:
        copy.wait()
    arrived = recv_buf[...].reshape(users * cap_pad, model)
    where_to = jnp.sum(jnp.where(diagonal, spot_in[...], 0.0), axis=2, keepdims=True)
    where_to = where_to.reshape(users * cap_pad, 1).astype(jnp.int32)
    placed = (
        lax.broadcasted_iota(jnp.int32, (users * cap_pad, block), 1) == where_to
    ).astype(F32).astype(BF16)
    sequence = dot(placed, arrived, (0, 0))
    seq_sc[...] = sequence.astype(BF16)
    normed = layer_norm(sequence)[0].astype(BF16)
    norm_sc[...] = normed
    projected = dot(normed, proj_w_ref[...]) + proj_b_ref[...]
    proj_sc[...] = projected
    gates = silu(projected).astype(BF16)
    gate_sc[...] = gates[:, :width]
    for p in range(pairs):
        low = p * LANES
        kv[me_s, p] = gates[:, 3 * width + low : 3 * width + low + LANES]
        kv[me_s, pairs + p] = gates[:, width + low : width + low + LANES]
        qb[me_s, p] = gates[:, 2 * width + low : 2 * width + low + LANES]

    steps = []
    bit = seqs // 2
    while bit >= 1:
        steps.append(bit)
        bit //= 2
    moves = []
    held = [0]
    for bit in steps:
        for delta in held:
            moves.append((delta, bit))
        held = held + [delta + bit for delta in held]

    def move(buf, send_sem, recv_sem, index):
        delta, bit = moves[index]
        held_block = flip_all(me_s, delta)
        peer = flip(me_s, bit)
        return (
            held_block,
            peer,
            pltpu.make_async_remote_copy(
                src_ref=buf.at[held_block],
                dst_ref=buf.at[held_block],
                send_sem=send_sem.at[index],
                recv_sem=recv_sem.at[delta + bit],
                device_id=(me_u, peer),
                device_id_type=MESH,
            ),
        )

    def arrive(buf, send_sem, recv_sem, delta):
        low_bit = delta & -delta
        source = flip_all(me_s, delta)
        pltpu.make_async_remote_copy(
            src_ref=buf.at[source],
            dst_ref=buf.at[source],
            send_sem=send_sem.at[0],
            recv_sem=recv_sem.at[delta],
            device_id=(me_u, flip(me_s, low_bit)),
            device_id_type=MESH,
        ).wait_recv()

    def up(held_block, peer):
        return held_block < peer

    def down(held_block, peer):
        return held_block > peer

    def start_own(buf, send_sem, recv_sem, way):
        for index, (delta, bit) in enumerate(moves):
            if delta == 0:
                held_block, peer, copy = move(buf, send_sem, recv_sem, index)

                @pl.when(way(held_block, peer))
                def _():
                    copy.start()

    def take(buf, send_sem, recv_sem, way, delta):
        source = flip_all(me_s, delta)

        @pl.when(way(source, me_s))
        def _():
            arrive(buf, send_sem, recv_sem, delta)
            for index, (held_delta, bit) in enumerate(moves):
                if held_delta == delta:
                    move(buf, send_sem, recv_sem, index)[2].start()

    def finish(buf, send_sem, recv_sem, way):
        for index in range(len(moves)):
            held_block, peer, copy = move(buf, send_sem, recv_sem, index)

            @pl.when(way(held_block, peer))
            def _():
                copy.wait_send()

    kv_set = (kv, kv_send, kv_recv, up)
    q_set = (qb, q_send, q_recv, down)
    g_set = (gb, g_send, g_recv, down)
    start_own(*kv_set)
    start_own(*q_set)

    lane_is_low = lax.broadcasted_iota(jnp.int32, (block, LANES), 1) < HEAD

    def half_of(values, hh):
        zero = jnp.zeros_like(values)
        return jnp.where(lane_is_low, values, zero) if hh == 0 else jnp.where(lane_is_low, zero, values)

    def scores_of(delta):
        other = flip_all(me_s, delta)
        q_index = jnp.maximum(other, me_s)
        k_index = jnp.minimum(other, me_s)
        bound = jnp.minimum(q_index * block + rows, length - 1) - k_index * block
        allowed = lax.broadcasted_iota(jnp.int32, (block, block), 1) <= bound
        for p in range(pairs):
            queries = qb[q_index, p]
            keys = kv[k_index, p]
            for hh in range(2):
                score = dot(half_of(queries, hh), keys, (1, 1)) * scale
                gate = sigmoid(score)
                plain = score * gate
                w_sc[delta, p, hh] = jnp.where(allowed, plain, 0.0).astype(BF16)
                s_sc[delta, p, hh] = jnp.where(allowed, gate + plain * (1.0 - gate), 0.0)

    def attend(delta):
        other = flip_all(me_s, delta)
        for p in range(pairs):
            values = kv[other, pairs + p]
            low = dot(w_sc[delta, p, 0], values)
            high = dot(w_sc[delta, p, 1], values)
            att[p] = att[p] + jnp.where(lane_is_low, low, high)

    att[...] = jnp.zeros_like(att)
    dq[...] = jnp.zeros_like(dq)
    dk[...] = jnp.zeros_like(dk)
    dv[...] = jnp.zeros_like(dv)
    scores_of(0)
    attend(0)
    for delta in range(1, seqs):
        other = flip_all(me_s, delta)
        take(*kv_set, delta)
        take(*q_set, delta)

        @pl.when(other < me_s)
        def _():
            scores_of(delta)
            attend(delta)

    attended = jnp.concatenate([att[p] for p in range(pairs)], axis=1)
    onorm, inverse = layer_norm(attended)
    gate_u = gate_sc[...].astype(F32)
    mixed = (onorm * gate_u).astype(BF16)
    d_mixed = dot(d_out, out_w_ref[...], (1, 1))
    d_gate_u = d_mixed * onorm
    d_onorm = d_mixed * gate_u
    d_att = (
        d_onorm
        - jnp.mean(d_onorm, axis=-1, keepdims=True)
        - onorm * jnp.mean(d_onorm * onorm, axis=-1, keepdims=True)
    ) * inverse
    d_att = d_att.astype(BF16)
    for p in range(pairs):
        gb[me_s, p] = d_att[:, p * LANES : (p + 1) * LANES]
    start_own(*g_set)
    projected_u = proj_sc[:, :width]
    dproj[:, :width] = (d_gate_u * silu_grad(projected_u)).astype(BF16)
    result = dot(mixed, out_w_ref[...]) + out_b_ref[...] + seq_sc[...].astype(F32)
    layer_ref[...] = jnp.where(present, result, 0.0).astype(BF16)
    bias[0] = jnp.zeros_like(bias[0])
    bias[0, 1:2, :model] = jnp.sum(d_out.astype(F32), axis=0, keepdims=True)
    (early, late), stages, total_chunks = plan_of(users, seqs, groups_of(model, width))
    late_base = late[0][0]

    def store_tiles(base, values):
        height = values.shape[0] // ROWS
        for tile in range(values.shape[1] // LANES):
            work[base + tile * height : base + (tile + 1) * height] = values[
                :, tile * LANES : (tile + 1) * LANES
            ].reshape(height, ROWS, LANES)
        return base + values.shape[0] * values.shape[1] // (ROWS * LANES)

    def clear(base, stop):
        if base < stop:
            work[base:stop] = jnp.zeros((stop - base, ROWS, LANES), BF16)

    filled = store_tiles(0, dot(mixed, d_out, (0, 0)).astype(BF16))
    filled = store_tiles(filled, dot(norm_sc[...], dproj[:, :width], (0, 0)).astype(BF16))
    clear(filled, late_base)

    def place_of(axis, bit):
        mine = me_s if axis == "seq" else me_u
        peer = flip(mine, bit)
        device = (me_u, peer) if axis == "seq" else (peer, me_s)
        return (mine // bit) % 2, device

    all_streams = early + late
    starts = [[base] for base, _, _ in all_streams]
    landings = []
    landing_at = 0
    for base, size, _ in all_streams:
        offsets = []
        for stage in range(stages):
            offsets.append(landing_at)
            landing_at += size >> (stage + 1)
        landings.append(offsets)
    early_ids = list(range(len(early)))
    late_ids = list(range(len(early), len(all_streams)))

    def reduce_copy(i, stage):
        base, size, bit_order = all_streams[i]
        side, device = place_of(*bit_order[stage])
        half = size >> (stage + 1)
        start = starts[i][stage]
        return (
            pltpu.make_async_remote_copy(
                src_ref=work.at[pl.ds(start + (1 - side) * half, half)],
                dst_ref=landing.at[pl.ds(landings[i][stage], half)],
                send_sem=rs_send.at[i, stage],
                recv_sem=rs_recv.at[i, stage],
                device_id=device,
                device_id_type=MESH,
            ),
            start + side * half,
            half,
        )

    def gather_copy(i, stage):
        base, size, bit_order = all_streams[i]
        _, device = place_of(*bit_order[stage])
        half = size >> (stage + 1)
        own = full.at[pl.ds(starts[i][stage + 1], half)]
        return pltpu.make_async_remote_copy(
            src_ref=own,
            dst_ref=own,
            send_sem=ag_send.at[i, stage],
            recv_sem=ag_recv.at[i, stage],
            device_id=device,
            device_id_type=MESH,
        )

    def reduce_start(ids):
        for i in ids:
            reduce_copy(i, 0)[0].start()

    def reduce_step(ids, stage):
        for i in ids:
            copy, keep, half = reduce_copy(i, stage)
            copy.wait()
            at = landings[i][stage]
            summed = (
                work[pl.ds(keep, half)].astype(F32) + landing[at : at + half].astype(F32)
            ).astype(BF16)
            starts[i].append(keep)
            if stage + 1 < stages:
                work[pl.ds(keep, half)] = summed
                reduce_copy(i, stage + 1)[0].start()
            else:
                full[pl.ds(keep, half)] = summed
                gather_copy(i, stage).start()

    def gather_step(ids, stage):
        for i in ids:
            gather_copy(i, stage).wait()
            if stage > 0:
                gather_copy(i, stage - 1).start()

    reduce_start(early_ids)

    for delta in range(1, seqs):
        other = flip_all(me_s, delta)

        @pl.when(other > me_s)
        def _():
            scores_of(delta)

    reduce_step(early_ids, 0)

    def backward(delta):
        other = flip_all(me_s, delta)
        q_index = jnp.maximum(other, me_s)
        k_index = jnp.minimum(other, me_s)
        for p in range(pairs):
            grads = gb[q_index, p]
            values = kv[k_index, pairs + p]
            d_scores = []
            for hh in range(2):
                d_weight = dot(half_of(grads, hh), values, (1, 1))
                d_scores.append((d_weight * s_sc[delta, p, hh]).astype(BF16))

            def query_side():
                keys = kv[k_index, p]
                dq[p] = dq[p] + jnp.where(
                    lane_is_low, dot(d_scores[0], keys), dot(d_scores[1], keys)
                )

            def key_side():
                queries = qb[q_index, p]
                dk[p] = dk[p] + jnp.where(
                    lane_is_low,
                    dot(d_scores[0], queries, (0, 0)),
                    dot(d_scores[1], queries, (0, 0)),
                )
                dv[p] = dv[p] + jnp.where(
                    lane_is_low,
                    dot(w_sc[delta, p, 0], grads, (0, 0)),
                    dot(w_sc[delta, p, 1], grads, (0, 0)),
                )

            if delta == 0:
                query_side()
                key_side()
            else:
                pl.when(other < me_s)(query_side)
                pl.when(other > me_s)(key_side)

    backward(0)
    for delta in range(1, seqs):
        other = flip_all(me_s, delta)

        @pl.when(other < me_s)
        def _():
            backward(delta)

    reduce_step(early_ids, 1)
    for delta in range(1, seqs):
        other = flip_all(me_s, delta)
        take(*g_set, delta)

        @pl.when(other > me_s)
        def _():
            backward(delta)

    reduce_step(early_ids, 2)
    early_done = 3
    for part, buf, factor in ((1, dv, 1.0), (2, dq, scale), (3, dk, scale)):
        slope = silu_grad(proj_sc[:, part * width : (part + 1) * width])
        for p in range(pairs):
            low = part * width + p * LANES
            dproj[:, low : low + LANES] = (
                buf[p] * factor * slope[:, p * LANES : (p + 1) * LANES]
            ).astype(BF16)

    d_proj = dproj[...]
    filled = store_tiles(late_base, dot(norm_sc[...], d_proj[:, width:], (0, 0)).astype(BF16))
    clear(filled, total_chunks)
    reduce_start(late_ids)
    bias[0, 0:1, :] = jnp.sum(d_proj.astype(F32), axis=0, keepdims=True)

    def bias_copy(stage):
        _, device = place_of(*all_streams[0][2][stage])
        return pltpu.make_async_remote_copy(
            src_ref=bias.at[stage],
            dst_ref=bias_in.at[stage],
            send_sem=b_send.at[stage],
            recv_sem=b_recv.at[stage],
            device_id=device,
            device_id_type=MESH,
        )

    def bias_step(stage):
        bias_copy(stage).wait()
        bias[stage + 1] = bias[stage] + bias_in[stage]
        if stage + 1 < stages:
            bias_copy(stage + 1).start()

    bias_copy(0).start()
    for turn in range(2 * stages):
        if turn < stages:
            reduce_step(late_ids, turn)
            bias_step(turn)
        else:
            gather_step(late_ids, 2 * stages - 1 - turn)
        ahead = turn + early_done
        if ahead < stages:
            reduce_step(early_ids, ahead)
        elif ahead < 2 * stages:
            gather_step(early_ids, 2 * stages - 1 - ahead)
    bias_ref[...] = bias[stages]
    finish(*kv_set)
    finish(*q_set)
    finish(*g_set)


def unpack(full, bias_ref, layer_in, layer_ref, gpw_ref, gpb_ref, gow_ref, gob_ref, late_base):
    model, width = gow_ref.shape[1], gow_ref.shape[0]
    layer_ref[...] = layer_in[...]
    gpb_ref[...] = bias_ref[0:1, :]
    gob_ref[...] = bias_ref[1:2, :model]

    def tile_of(base, height):
        return full[base : base + height // ROWS].reshape(height, LANES)

    at = 0
    for tile in range(model // LANES):
        gow_ref[:, tile * LANES : (tile + 1) * LANES] = tile_of(at, width)
        at += width // ROWS
    for tile in range(4 * width // LANES):
        if tile == width // LANES:
            at = late_base
        gpw_ref[:, tile * LANES : (tile + 1) * LANES] = tile_of(at, model)
        at += model // ROWS


def on_device(
    users,
    seqs,
    raw_events,
    target_user,
    target_place,
    send_counts,
    lengths,
    cotangent,
    encoder_in,
    encoder_out,
    proj_weight,
    proj_bias,
    out_weight,
    out_bias,
):
    slots = raw_events.shape[1]
    block, model = cotangent.shape[1], cotangent.shape[2]
    width = out_weight.shape[0]
    pairs = width // LANES
    cap_pad = -(-(slots // users) // ROWS) * ROWS
    (early, late), stages, total = plan_of(users, seqs, groups_of(model, width))
    count = len(early) + len(late)
    vmem = pl.BlockSpec(memory_space=pltpu.VMEM)
    anywhere = pl.BlockSpec(memory_space=pl.ANY)
    smem = pl.BlockSpec(memory_space=pltpu.SMEM)
    dma = pltpu.SemaphoreType.DMA
    moves = seqs - 1
    layer, full, bias = pl.pallas_call(
        functools.partial(kernel, users, seqs),
        out_shape=(
            jax.ShapeDtypeStruct((block, model), BF16),
            jax.ShapeDtypeStruct((total, ROWS, LANES), BF16),
            jax.ShapeDtypeStruct((2, 4 * width), F32),
        ),
        in_specs=[anywhere, vmem, vmem, smem, smem] + [anywhere] * 4 + [vmem, anywhere, vmem],
        out_specs=(vmem,) * 3,
        scratch_shapes=[
            pltpu.VMEM((users, cap_pad, model), BF16),
            pltpu.VMEM((users, cap_pad, model), BF16),
            pltpu.VMEM((users, 1, LANES), F32),
            pltpu.VMEM((users, 1, LANES), F32),
            pltpu.VMEM((block, model), BF16),
            pltpu.VMEM((block, model), BF16),
            pltpu.VMEM((block, 4 * width), F32),
            pltpu.VMEM((block, width), BF16),
            pltpu.VMEM((seqs, 2 * pairs, block, LANES), BF16),
            pltpu.VMEM((seqs, pairs, block, LANES), BF16),
            pltpu.VMEM((seqs, pairs, block, LANES), BF16),
            pltpu.VMEM((seqs, pairs, 2, block, block), BF16),
            pltpu.VMEM((seqs, pairs, 2, block, block), F32),
            pltpu.VMEM((pairs, block, LANES), F32),
            pltpu.VMEM((pairs, block, LANES), F32),
            pltpu.VMEM((pairs, block, LANES), F32),
            pltpu.VMEM((pairs, block, LANES), F32),
            pltpu.VMEM((block, 4 * width), BF16),
            pltpu.VMEM((total, ROWS, LANES), BF16),
            pltpu.VMEM((total, ROWS, LANES), BF16),
            pltpu.VMEM((stages + 1, 2, 4 * width), F32),
            pltpu.VMEM((stages, 2, 4 * width), F32),
            dma((users,)),
            dma((users,)),
            dma((users,)),
            dma((users,)),
            dma((moves,)),
            dma((seqs,)),
            dma((moves,)),
            dma((seqs,)),
            dma((moves,)),
            dma((seqs,)),
            dma((count, stages)),
            dma((count, stages)),
            dma((count, stages)),
            dma((count, stages)),
            dma((stages,)),
            dma((stages,)),
            pltpu.VMEM(raw_events.shape[1:], BF16),
            pltpu.VMEM(cotangent.shape[1:], BF16),
            pltpu.VMEM(encoder_in.shape, BF16),
            pltpu.VMEM(encoder_out.shape, BF16),
            pltpu.VMEM(proj_weight.shape, BF16),
            pltpu.VMEM(out_weight.shape, BF16),
            dma((6,)),
        ],
        compiler_params=pltpu.CompilerParams(
            collective_id=0, has_side_effects=True, vmem_limit_bytes=60000 * 1024
        ),
    )(
        raw_events[0],
        target_user,
        target_place,
        send_counts[0],
        lengths,
        cotangent[0],
        encoder_in,
        encoder_out,
        proj_weight,
        proj_bias[None],
        out_weight,
        out_bias[None],
    )
    layer_out, grad_pw, grad_pb, grad_ow, grad_ob = pl.pallas_call(
        functools.partial(unpack, late_base=late[0][0]),
        out_shape=(
            jax.ShapeDtypeStruct((block, model), BF16),
            jax.ShapeDtypeStruct((model, 4 * width), BF16),
            jax.ShapeDtypeStruct((1, 4 * width), F32),
            jax.ShapeDtypeStruct((width, model), BF16),
            jax.ShapeDtypeStruct((1, model), F32),
        ),
        in_specs=[vmem] * 3,
        out_specs=(vmem,) * 5,
    )(full, bias, layer)
    return layer_out[None], grad_pw, grad_pb[0], grad_ow, grad_ob[0]


def solution(mesh):
    placed = (
        P("seq", "users", None),
        P("seq", "users"),
        P("seq", "users"),
        P("seq", "users", None),
        P("users"),
        P("users", "seq", None),
        P(),
        P(),
        P(),
        P(),
        P(),
        P(),
    )
    return jax.shard_map(
        functools.partial(on_device, mesh.shape["users"], mesh.shape["seq"]),
        mesh=mesh,
        in_specs=placed,
        out_specs=(P("users", "seq", None), P(), P(), P(), P()),
        check_vma=False,
    )
```
